32 devices in a mesh: lat: 8 (over z, y), lon: 4 (over x, core).
Axes of the slice: x: 2, y: 2, z: 4, core: 2. Of those that a mesh axis runs over, the one named last changes fastest.
Arguments:
- grid_feat: bfloat16 [32768, 512], P(('lat', 'lon')), may hold values from -6 to 6
- mesh_feat: bfloat16 [2048, 512], P(('lat', 'lon')), may hold values from -6 to 6
- enc_send: int32 [32, 9, 256], P(('lat', 'lon')), may hold values from 0 to 1023
- enc_recv: int32 [32, 9, 256], P(('lat', 'lon')), may hold values from 0 to 63
- enc_count: int32 [32, 9], P(('lat', 'lon')), may hold values from 0 to 256, as said below
- dec_send: int32 [32, 9, 512], P(('lat', 'lon')), may hold values from 0 to 63
- dec_recv: int32 [32, 9, 512], P(('lat', 'lon')), may hold values from 0 to 1023
- dec_count: int32 [32, 9], P(('lat', 'lon')), may hold values from 0 to 512, as said below
- enc_src: bfloat16 [512, 512], replicated, may hold values from -0.25 to 0.25
- enc_dst: bfloat16 [512, 512], replicated, may hold values from -0.25 to 0.25
- enc_bias: float32 [512], replicated, may hold values from -3 to 3
- enc_out: bfloat16 [512, 512], replicated, may hold values from -0.03125 to 0.03125
- dec_src: bfloat16 [512, 512], replicated, may hold values from -0.25 to 0.25
- dec_dst: bfloat16 [512, 512], replicated, may hold values from -0.25 to 0.25
- dec_bias: float32 [512], replicated, may hold values from -3 to 3
- dec_out: bfloat16 [512, 512], replicated, may hold values from -0.1875 to 0.1875
- grid_cot: bfloat16 [32768, 512], P(('lat', 'lon')), may hold values from -6 to 6
Outputs:
- grid_new: bfloat16 [32768, 512], P(('lat', 'lon'))
- mesh_grad: bfloat16 [2048, 512], P(('lat', 'lon'))
- grid_grad: bfloat16 [32768, 512], P(('lat', 'lon'))
The draws below stay inside these ranges and needn't reach their ends.
Inputs may be any that keep to these rules, and one draw needn't show every extreme that they name: `enc_send`: row of the grid device's own tile. `enc_recv`: row of the mesh tile of the block's neighbour. `enc_count`: live slots of each block; 0 where the neighbour would lie beyond a pole; block 4 (the device itself) is full, and in every draw some device receives full blocks from all its neighbours. `dec_send`: row of the mesh tile of the block's neighbour. `dec_recv`: row of the grid device's own tile. `dec_count`: live slots of each block; 0 where the neighbour would lie beyond a pole; block 4 (the device itself) is full, and in every draw some device sends full blocks to all its neighbours.
All inputs are finite; a program needn't handle non-finite values.
Results may differ from the reference program's by a relative error of at most 0.0086.
Values may be sent and summed in bfloat16 or wider, within the bound.
A program may use at most 128 MiB of HBM per device.

```python
import jax
import jax.numpy as jnp
from jax import lax

D = 512
G_DEV = 1024
M_DEV = 64
CAP_E = 256
CAP_D = 512
OWNERS = 32
GRID = 32768
MESH = 2048
N_LAT = 8
N_LON = 4


def neighbour_counts(key, capacity):
    owners = jnp.arange(OWNERS, dtype=jnp.int32)
    offsets = jnp.arange(9, dtype=jnp.int32)
    lat_band = owners // N_LON
    lon_sector = owners % N_LON
    target_band = lat_band[:, None] + offsets[None, :] // 3 - 1
    target_sector = (lon_sector[:, None] + offsets[None, :] % 3 - 1) % N_LON
    inside = (target_band >= 0) & (target_band < N_LAT)
    target = jnp.clip(target_band, 0, N_LAT - 1) * N_LON + target_sector
    polar_band = (lat_band == 0) | (lat_band == N_LAT - 1)
    quiet_key, busy_key, busiest_key = jax.random.split(key, 3)
    quiet_load = jax.random.randint(quiet_key, (OWNERS, 9), capacity // 4, 3 * capacity // 4 + 1)
    busy_load = jax.random.randint(busy_key, (OWNERS, 9), capacity // 2, capacity + 1)
    counts = jnp.where(polar_band[:, None], busy_load, quiet_load)
    busiest = jax.random.randint(busiest_key, (), 0, OWNERS)
    filled = (offsets[None, :] == 4) | (target == busiest)
    counts = jnp.where(filled, capacity, counts)
    counts = jnp.where(inside, counts, 0)
    return counts.astype(jnp.int32)


def draw_enc_count(key, part):
    return neighbour_counts(jax.random.fold_in(key, 11), CAP_E)


def draw_dec_count(key, part):
    return neighbour_counts(jax.random.fold_in(key, 23), CAP_D)


def with_ends(result, own_key, least, high):
    spot = [jax.random.randint(jax.random.fold_in(own_key, axis), (), 0, length) for axis, length in enumerate(result.shape)]
    longest = result.shape.index(max(result.shape))
    neighbour = spot[:longest] + [(spot[longest] + 1) % result.shape[longest]] + spot[longest + 1:]
    return result.at[tuple(spot)].set(least).at[tuple(neighbour)].set(high)


def steps_of(stream_key, extent, cuts, least, largest):
    gain = 1.0
    for axis_at, shards_of in cuts:
        steps = jax.random.uniform(jax.random.fold_in(jax.random.fold_in(stream_key, 6), axis_at), (shards_of,), jnp.float32, least / len(cuts), largest / len(cuts))
        gain = gain * jnp.repeat(jnp.exp(steps), extent[axis_at] // shards_of).reshape((-1,) + (1,) * (len(extent) - 1 - axis_at))
    return gain


def normal_values(rng, dims, scale, bound, shards=(), kind=jnp.bfloat16):
    factor_of = steps_of(rng, dims, shards, -0.22, 0.18) if shards else 1.0
    values = jax.random.normal(rng, dims, jnp.float32) * scale * factor_of
    return jnp.minimum(jnp.maximum(values, -bound), bound).astype(kind)


def setup_inputs(seed: int = 0) -> dict:
    splits = jax.random.split(jax.random.key(seed), 18)
    return {
        "grid_feat": normal_values(splits[0], (GRID, D), 1.0, 6.0, ((0, 32),)),
        "mesh_feat": normal_values(splits[1], (MESH, D), 1.0, 6.0, ((0, 32),)),
        "enc_send": with_ends(jax.random.randint(splits[2], (OWNERS, 9, CAP_E), 0, G_DEV), jax.random.fold_in(splits[2], 1), 0, G_DEV - 1).astype(jnp.int32),
        "enc_recv": with_ends(jax.random.randint(splits[3], (OWNERS, 9, CAP_E), 0, M_DEV), jax.random.fold_in(splits[3], 1), 0, M_DEV - 1).astype(jnp.int32),
        "enc_count": draw_enc_count(jax.random.fold_in(splits[17], 71), 0),
        "dec_send": with_ends(jax.random.randint(splits[5], (OWNERS, 9, CAP_D), 0, M_DEV), jax.random.fold_in(splits[5], 1), 0, M_DEV - 1).astype(jnp.int32),
        "dec_recv": with_ends(jax.random.randint(splits[6], (OWNERS, 9, CAP_D), 0, G_DEV), jax.random.fold_in(splits[6], 1), 0, G_DEV - 1).astype(jnp.int32),
        "dec_count": draw_dec_count(jax.random.fold_in(splits[17], 71), 0),
        "enc_src": normal_values(splits[8], (D, D), D ** -0.5, 0.25),
        "enc_dst": normal_values(splits[9], (D, D), D ** -0.5, 0.25),
        "enc_bias": normal_values(splits[10], (D,), 0.5, 3.0, (), jnp.float32),
        "enc_out": normal_values(splits[11], (D, D), (D * 64) ** -0.5, 0.03125),
        "dec_src": normal_values(splits[12], (D, D), D ** -0.5, 0.25),
        "dec_dst": normal_values(splits[13], (D, D), D ** -0.5, 0.25),
        "dec_bias": normal_values(splits[14], (D,), 0.5, 3.0, (), jnp.float32),
        "dec_out": normal_values(splits[15], (D, D), (D * 2) ** -0.5, 0.1875),
        "grid_cot": normal_values(splits[16], (GRID, D), 1.0, 6.0, ((0, 32),)),
    }


def silu_slope(pre_act):
    squashed = jax.nn.sigmoid(pre_act)
    return squashed * (1.0 + pre_act * (1.0 - squashed))


def slot_keep(counts, capacity):
    slot_index = jnp.arange(capacity, dtype=jnp.int32)
    return (slot_index[None, :] < counts[:, None]).astype(jnp.float32)[..., None]


def rounded(values):
    return lax.optimization_barrier(values.astype(jnp.bfloat16)).astype(jnp.float32)


def neighbour_owners():
    owners = jnp.arange(OWNERS, dtype=jnp.int32)
    offsets = jnp.arange(9, dtype=jnp.int32)
    lat_band = owners // N_LON
    lon_sector = owners % N_LON
    target_band = jnp.clip(lat_band[:, None] + offsets[None, :] // 3 - 1, 0, N_LAT - 1)
    target_sector = (lon_sector[:, None] + offsets[None, :] % 3 - 1) % N_LON
    return (target_band * N_LON + target_sector).astype(jnp.int32)


def reference(grid_feat, mesh_feat, enc_send, enc_recv, enc_count, dec_send, dec_recv, dec_count, enc_src, enc_dst, enc_bias, enc_out, dec_src, dec_dst, dec_bias, dec_out, grid_cot):
    owners = jnp.arange(OWNERS, dtype=jnp.int32)
    neighbours = neighbour_owners()
    enc_proj = jnp.dot(grid_feat, enc_src, preferred_element_type=jnp.float32).astype(jnp.bfloat16).reshape(OWNERS, G_DEV, D)
    mesh_side = jnp.dot(mesh_feat, enc_dst, preferred_element_type=jnp.float32)

    def enc_edges(device):
        senders = enc_proj[device][enc_send[device]]
        receivers = (neighbours[device][:, None] * M_DEV + enc_recv[device]).astype(jnp.int32)
        pre_act = senders.astype(jnp.float32) + mesh_side[receivers] + enc_bias
        return pre_act, slot_keep(enc_count[device], CAP_E), receivers

    def enc_forward(running, device):
        pre_act, keeper, receivers = enc_edges(device)
        flat_msg = rounded(jax.nn.silu(pre_act) * keeper).reshape(-1, D)
        return running.at[receivers.reshape(-1)].add(flat_msg), None

    enc_total, _ = lax.scan(enc_forward, jnp.zeros((MESH, D), jnp.float32), owners)
    enc_sum = enc_total.astype(jnp.bfloat16)
    mesh_new = (mesh_feat.astype(jnp.float32) + jnp.dot(enc_sum, enc_out, preferred_element_type=jnp.float32)).astype(jnp.bfloat16)

    dec_proj = jnp.dot(mesh_new, dec_src, preferred_element_type=jnp.float32).astype(jnp.bfloat16)
    grid_side = jnp.dot(grid_feat, dec_dst, preferred_element_type=jnp.float32).reshape(OWNERS, G_DEV, D)

    def dec_edges(device):
        senders = (neighbours[device][:, None] * M_DEV + dec_send[device]).astype(jnp.int32)
        receivers = dec_recv[device]
        pre_act = dec_proj[senders].astype(jnp.float32) + grid_side[device][receivers] + dec_bias
        return pre_act, slot_keep(dec_count[device], CAP_D), senders, receivers

    def dec_forward(device):
        pre_act, keeper, senders, receivers = dec_edges(device)
        flat_msg = rounded(jax.nn.silu(pre_act) * keeper).reshape(-1, D)
        summed = jax.ops.segment_sum(flat_msg, receivers.reshape(-1), num_segments=G_DEV)
        return summed.astype(jnp.bfloat16)

    dec_sum = lax.map(dec_forward, owners).reshape(GRID, D)
    grid_new = (grid_feat.astype(jnp.float32) + jnp.dot(dec_sum, dec_out, preferred_element_type=jnp.float32)).astype(jnp.bfloat16)

    grid_back = jnp.dot(grid_cot, dec_out.T, preferred_element_type=jnp.float32).astype(jnp.bfloat16).reshape(OWNERS, G_DEV, D)

    def dec_backward(running, device):
        pre_act, keeper, senders, receivers = dec_edges(device)
        flat_grad = rounded(grid_back[device][receivers].astype(jnp.float32) * silu_slope(pre_act) * keeper).reshape(-1, D)
        local_sum = jax.ops.segment_sum(flat_grad, receivers.reshape(-1), num_segments=G_DEV).astype(jnp.bfloat16)
        return running.at[senders.reshape(-1)].add(flat_grad), local_sum

    mesh_total, dec_local = lax.scan(dec_backward, jnp.zeros((MESH, D), jnp.float32), owners)
    dec_grid = jnp.dot(dec_local.reshape(GRID, D), dec_dst.T, preferred_element_type=jnp.float32)
    mesh_back = jnp.dot(mesh_total.astype(jnp.bfloat16), dec_src.T, preferred_element_type=jnp.float32)
    enc_back = jnp.dot(mesh_back.astype(jnp.bfloat16), enc_out.T, preferred_element_type=jnp.float32).astype(jnp.bfloat16)

    def enc_backward(running, device):
        pre_act, keeper, receivers = enc_edges(device)
        flat_grad = rounded(enc_back[receivers].astype(jnp.float32) * silu_slope(pre_act) * keeper).reshape(-1, D)
        local_sum = jax.ops.segment_sum(flat_grad, enc_send[device].reshape(-1), num_segments=G_DEV).astype(jnp.bfloat16)
        return running.at[receivers.reshape(-1)].add(flat_grad), local_sum

    enc_local, grid_total = lax.scan(enc_backward, jnp.zeros((MESH, D), jnp.float32), owners)
    mesh_grad = (mesh_back + jnp.dot(enc_local.astype(jnp.bfloat16), enc_dst.T, preferred_element_type=jnp.float32)).astype(jnp.bfloat16)
    enc_grid = jnp.dot(grid_total.reshape(GRID, D), enc_src.T, preferred_element_type=jnp.float32)
    grid_grad = (grid_cot.astype(jnp.float32) + dec_grid + enc_grid).astype(jnp.bfloat16)
    return grid_new, mesh_grad, grid_grad
```

```python
import functools

import jax
import jax.numpy as jnp
from jax import lax
from jax.experimental import pallas as pl
from jax.experimental.pallas import tpu as pltpu
from jax.sharding import PartitionSpec as P

F32 = jnp.float32
BF16 = jnp.bfloat16
MESH = pl.DeviceIdType.MESH


def mm(a, b):
    return jnp.dot(a, b, preferred_element_type=F32)


def mm_t(a, b):
    return lax.dot_general(a, b, (((1,), (1,)), ((), ())), preferred_element_type=F32)


def lane_row(width):
    return lax.broadcasted_iota(jnp.int32, (1, width), 1)


def ones_where(mask):
    return jnp.where(mask, 1.0, 0.0).astype(BF16)


def pick_columns(column, row_count):
    return ones_where(column == lane_row(row_count).astype(F32))


def pick_rows(indices, row_count, base=0):
    rows = lax.broadcasted_iota(jnp.int32, (row_count, 1), 0) + base
    return ones_where(rows == indices)


def column_of(columns_ref, at):
    columns = columns_ref[...]
    lane = lax.broadcasted_iota(jnp.int32, columns.shape, 1)
    return jnp.sum(jnp.where(lane == at, columns, 0.0), axis=1, keepdims=True)


def live_row(index_ref, count_ref, k):
    indices = index_ref[pl.ds(k, 1), :]
    return jnp.where(lane_row(indices.shape[1]) < count_ref[0, k], indices, -1)


def gate_of(pre):
    return 0.5 * jnp.tanh(0.5 * pre) + 0.5


def kernel(
    n_lat,
    n_lon,
    grid_feat,
    mesh_feat,
    enc_send,
    enc_recv,
    enc_count,
    dec_send,
    dec_recv,
    dec_count,
    enc_columns,
    dec_columns,
    enc_src,
    enc_dst,
    enc_bias,
    enc_out,
    dec_src,
    dec_dst,
    dec_bias,
    dec_out,
    grid_cot,
    grid_new,
    mesh_grad,
    grid_grad,
    enc_table,
    dec_table,
    enc_edges,
    enc_slope,
    dec_edges,
    grid_part,
    mesh_back,
    tile_out,
    part_out,
    landed,
    send_sem,
    recv_sem,
):
    lat = lax.axis_index("lat")
    lon = lax.axis_index("lon")
    grid_rows, width = grid_feat.shape
    mesh_rows = mesh_feat.shape[0]
    enc_cap = enc_send.shape[1]
    dec_cap = dec_send.shape[1]
    others = (0, 2, 6, 8, 1, 7, 3, 5)

    def inside(k):
        band = lat + k // 3 - 1
        return (band >= 0) & (band < n_lat)

    def peer(k):
        return (lat + k // 3 - 1, lax.rem(lon + k % 3 - 1 + n_lon, n_lon))

    def copy_of(stage, source, k):
        return pltpu.make_async_remote_copy(
            src_ref=source,
            dst_ref=landed.at[stage, 8 - k],
            send_sem=send_sem.at[stage, k],
            recv_sem=recv_sem.at[stage, 8 - k],
            device_id=peer(k),
            device_id_type=MESH,
        )

    def spread(stage, source):
        for k in others:

            @pl.when(inside(k))
            def _():
                copy_of(stage, source, k).start()

    def fold_out(stage, part, k):
        @pl.when((k != 4) & inside(k))
        def _():
            copy_of(stage, part_out.at[part, k], k).start()

    def arrived(stage, source):
        for k in others:

            @pl.when(inside(k))
            def _():
                copy_of(stage, source, 8 - k).wait_recv()

    def folded(stage, part):
        arrived(stage, part_out.at[part, 0])
        total = part_out[part, 4].astype(F32)
        for k in others:
            total = total + landed[stage, k].astype(F32)
        return total.astype(BF16)

    barrier = pltpu.get_barrier_semaphore()
    for k in others:

        @pl.when(inside(k))
        def _():
            pl.semaphore_signal(barrier, inc=1, device_id=peer(k), device_id_type=MESH)

    missing = jnp.where(lat == 0, 3, 0) + jnp.where(lat == n_lat - 1, 3, 0)
    pl.semaphore_wait(barrier, 8 - missing)

    spread(0, mesh_feat)

    for k in (0, 1, 2, 6, 7, 8):

        @pl.when(jnp.logical_not(inside(k)))
        def _():
            for stage in range(6):
                landed[stage, k] = jnp.zeros((mesh_rows, width), BF16)

    landed[0, 4] = mesh_feat[...]

    chunk = min(256, grid_rows)

    def rows_at(i, size):
        return pl.ds(pl.multiple_of(i * size, size), size)

    def project(i, _):
        rows = rows_at(i, chunk)
        enc_table[rows, :] = mm(grid_feat[rows, :], enc_src[...]).astype(BF16)
        dec_table[rows, :width] = mm(grid_feat[rows, :], dec_dst[...]).astype(BF16)
        dec_table[rows, width:] = mm_t(grid_cot[rows, :], dec_out[...]).astype(BF16)
        return 0

    lax.fori_loop(0, grid_rows // chunk, project, 0)

    def enc_gather(k, _):
        picks = pick_columns(column_of(enc_columns, k), grid_rows)
        enc_edges[rows_at(k, enc_cap), :] = mm(picks, enc_table[...]).astype(BF16)
        return 0

    lax.fori_loop(0, 9, enc_gather, 0)

    arrived(0, mesh_feat)

    def enc_forward(k, _):
        rows = rows_at(k, enc_cap)
        side = mm(landed[0, k], enc_dst[...])
        high = side.astype(BF16)
        low = (side - high.astype(F32)).astype(BF16)
        picks = pick_columns(column_of(enc_columns, k + 9), mesh_rows)
        near = mm(picks, high) + mm(picks, low)
        pre = enc_edges[rows, :].astype(F32) + near + enc_bias[...]
        gate = gate_of(pre)
        message = pre * gate
        enc_slope[rows, :] = gate + message * (1.0 - gate)
        targets = pick_rows(live_row(enc_recv, enc_count, k), mesh_rows)
        part_out[0, k] = mm(targets, message.astype(BF16)).astype(BF16)
        fold_out(1, 0, k)
        return 0

    lax.fori_loop(0, 9, enc_forward, 0)

    def dec_gather(k, _):
        picks = pick_columns(column_of(dec_columns, k + 9), grid_rows)
        dec_edges[rows_at(k, dec_cap), :] = mm(picks, dec_table[...]).astype(BF16)
        return 0

    lax.fori_loop(0, 5, dec_gather, 0)

    enc_sum = folded(1, 0)
    mesh_new = (mesh_feat[...].astype(F32) + mm(enc_sum, enc_out[...])).astype(BF16)
    dec_proj = mm(mesh_new, dec_src[...]).astype(BF16)
    tile_out[0] = dec_proj
    landed[2, 4] = dec_proj
    spread(2, tile_out.at[0])

    lax.fori_loop(5, 9, dec_gather, 0)

    arrived(2, tile_out.at[0])
    step = min(256, dec_cap)

    def dec_forward(k, _):
        near_picks = pick_columns(column_of(dec_columns, k), mesh_rows)
        near = landed[2, k]
        for first in range(0, dec_cap, step):
            rows = pl.ds(pl.multiple_of(k * dec_cap + first, step), step)
            pre = (
                mm(near_picks[first : first + step], near)
                + dec_edges[rows, :width].astype(F32)
                + dec_bias[...]
            )
            gate = gate_of(pre)
            message = pre * gate
            slope = gate + message * (1.0 - gate)
            back = dec_edges[rows, width:].astype(F32)
            dec_edges[rows, :width] = message.astype(BF16)
            dec_edges[rows, width:] = (back * slope).astype(BF16)
        targets = pick_rows(live_row(dec_send, dec_count, k), mesh_rows)
        part_out[1, k] = mm(targets, dec_edges[rows_at(k, dec_cap), width:]).astype(BF16)
        fold_out(3, 1, k)
        return 0

    lax.fori_loop(0, 9, dec_forward, 0)

    def dec_scatter(i, _):
        rows = rows_at(i, chunk)
        targets = jnp.concatenate(
            [pick_rows(live_row(dec_recv, dec_count, k), chunk, i * chunk) for k in range(9)], axis=1
        )
        summed = mm(targets, dec_edges[...]).astype(BF16)
        grid_new[rows, :] = (
            grid_feat[rows, :].astype(F32) + mm(summed[:, :width], dec_out[...])
        ).astype(BF16)
        grid_part[rows, :] = grid_cot[rows, :].astype(F32) + mm_t(summed[:, width:], dec_dst[...])
        return 0

    half = (grid_rows // chunk + 1) // 2
    lax.fori_loop(0, half, dec_scatter, 0)

    back = mm_t(folded(3, 1), dec_src[...])
    mesh_back[...] = back
    enc_back = mm_t(back.astype(BF16), enc_out[...]).astype(BF16)
    tile_out[1] = enc_back
    landed[4, 4] = enc_back
    spread(4, tile_out.at[1])

    lax.fori_loop(half, grid_rows // chunk, dec_scatter, 0)

    arrived(4, tile_out.at[1])

    def enc_backward(k, _):
        rows = rows_at(k, enc_cap)
        picks = pick_columns(column_of(enc_columns, k + 9), mesh_rows)
        grad = (mm(picks, landed[4, k]) * enc_slope[rows, :]).astype(BF16)
        enc_edges[rows, :] = grad
        targets = pick_rows(live_row(enc_recv, enc_count, k), mesh_rows)
        part_out[2, k] = mm(targets, grad).astype(BF16)
        fold_out(5, 2, k)
        return 0

    lax.fori_loop(0, 9, enc_backward, 0)

    def enc_scatter(i, _):
        rows = rows_at(i, chunk)
        targets = jnp.concatenate(
            [pick_rows(live_row(enc_send, enc_count, k), chunk, i * chunk) for k in range(9)], axis=1
        )
        summed = mm(targets, enc_edges[...]).astype(BF16)
        grid_grad[rows, :] = (grid_part[rows, :] + mm_t(summed, enc_src[...])).astype(BF16)
        return 0

    lax.fori_loop(0, grid_rows // chunk, enc_scatter, 0)

    mesh_grad[...] = (mesh_back[...] + mm_t(folded(5, 2), enc_dst[...])).astype(BF16)

    for k in others:

        @pl.when(inside(k))
        def _():
            copy_of(0, mesh_feat, k).wait_send()
            copy_of(1, part_out.at[0, k], k).wait_send()
            copy_of(2, tile_out.at[0], k).wait_send()
            copy_of(3, part_out.at[1, k], k).wait_send()
            copy_of(4, tile_out.at[1], k).wait_send()
            copy_of(5, part_out.at[2, k], k).wait_send()


def on_device(
    n_lat,
    n_lon,
    grid_feat,
    mesh_feat,
    enc_send,
    enc_recv,
    enc_count,
    dec_send,
    dec_recv,
    dec_count,
    enc_src,
    enc_dst,
    enc_bias,
    enc_out,
    dec_src,
    dec_dst,
    dec_bias,
    dec_out,
    grid_cot,
):
    grid_rows, width = grid_feat.shape
    mesh_rows = mesh_feat.shape[0]
    enc_slots = 9 * enc_send.shape[2]
    dec_slots = 9 * dec_send.shape[2]
    enc_columns = jnp.concatenate([enc_send[0], enc_recv[0]], axis=0).T.astype(F32)
    dec_columns = jnp.concatenate([dec_send[0], dec_recv[0]], axis=0).T.astype(F32)
    vmem = pl.BlockSpec(memory_space=pltpu.VMEM)
    smem = pl.BlockSpec(memory_space=pltpu.SMEM)
    return pl.pallas_call(
        functools.partial(kernel, n_lat, n_lon),
        out_shape=(
            jax.ShapeDtypeStruct((grid_rows, width), BF16),
            jax.ShapeDtypeStruct((mesh_rows, width), BF16),
            jax.ShapeDtypeStruct((grid_rows, width), BF16),
        ),
        in_specs=[vmem] * 4 + [smem] + [vmem] * 2 + [smem] + [vmem] * 11,
        out_specs=(vmem, vmem, vmem),
        scratch_shapes=[
            pltpu.VMEM((grid_rows, width), BF16),
            pltpu.VMEM((grid_rows, 2 * width), BF16),
            pltpu.VMEM((enc_slots, width), BF16),
            pltpu.VMEM((enc_slots, width), F32),
            pltpu.VMEM((dec_slots, 2 * width), BF16),
            pltpu.VMEM((grid_rows, width), F32),
            pltpu.VMEM((mesh_rows, width), F32),
            pltpu.VMEM((2, mesh_rows, width), BF16),
            pltpu.VMEM((3, 9, mesh_rows, width), BF16),
            pltpu.VMEM((6, 9, mesh_rows, width), BF16),
            pltpu.SemaphoreType.DMA((6, 9)),
            pltpu.SemaphoreType.DMA((6, 9)),
        ],
        compiler_params=pltpu.CompilerParams(
            collective_id=0, has_side_effects=True, vmem_limit_bytes=60 * 1024 * 1024
        ),
    )(
        grid_feat,
        mesh_feat,
        enc_send[0],
        enc_recv[0],
        enc_count,
        dec_send[0],
        dec_recv[0],
        dec_count,
        enc_columns,
        dec_columns,
        enc_src,
        enc_dst,
        enc_bias[None, :],
        enc_out,
        dec_src,
        dec_dst,
        dec_bias[None, :],
        dec_out,
        grid_cot,
    )


def solution(mesh):
    owned2 = P(("lat", "lon"), None)
    owned3 = P(("lat", "lon"), None, None)
    placed = (owned2, owned2, owned3, owned3, owned2, owned3, owned3, owned2) + (P(),) * 8 + (owned2,)
    return jax.shard_map(
        functools.partial(on_device, mesh.shape["lat"], mesh.shape["lon"]),
        mesh=mesh,
        in_specs=placed,
        out_specs=(owned2, owned2, owned2),
        check_vma=False,
    )
```

```python
import functools

import jax
import jax.numpy as jnp
from jax import lax
from jax.experimental import pallas as pl
from jax.experimental.pallas import tpu as pltpu
from jax.sharding import PartitionSpec as P

F32 = jnp.float32
BF16 = jnp.bfloat16
MESH = pl.DeviceIdType.MESH


def mm(a, b):
    return jnp.dot(a, b, preferred_element_type=F32)


def mm_t(a, b):
    return lax.dot_general(a, b, (((1,), (1,)), ((), ())), preferred_element_type=F32)


def lane_row(width):
    return lax.broadcasted_iota(jnp.int32, (1, width), 1)


def ones_where(mask):
    return jnp.where(mask, 1.0, 0.0).astype(BF16)


def pick_columns(column, row_count):
    return ones_where(column == lane_row(row_count).astype(F32))


def pick_rows(indices, row_count, base=0):
    rows = lax.broadcasted_iota(jnp.int32, (row_count, 1), 0) + base
    return ones_where(rows == indices)


def lay_columns(index_ref, columns_ref, at):
    blocks, _, slots = index_ref.shape
    rows = [index_ref[k].astype(F32) for k in range(blocks)]
    rows.append(jnp.zeros((16 - blocks, slots), F32))
    columns_ref[at] = jnp.concatenate(rows, axis=0).T


def column_of(columns_ref, which, at):
    columns = columns_ref[which]
    lane = lax.broadcasted_iota(jnp.int32, columns.shape, 1)
    return jnp.sum(jnp.where(lane == at, columns, 0.0), axis=1, keepdims=True)


def live_row(index_ref, count_ref, k):
    indices = index_ref[k]
    return jnp.where(lane_row(indices.shape[1]) < count_ref[0, k], indices, -1)


def gate_of(pre):
    return 0.5 * jnp.tanh(0.5 * pre) + 0.5


def kernel(
    n_lat,
    n_lon,
    grid_feat,
    mesh_feat,
    enc_send,
    enc_recv,
    enc_count,
    dec_send,
    dec_recv,
    dec_count,
    enc_src,
    enc_dst,
    enc_bias,
    enc_out,
    dec_src,
    dec_dst,
    dec_bias,
    dec_out,
    grid_cot,
    grid_new,
    mesh_grad,
    grid_grad,
    enc_table,
    dec_table,
    enc_edges,
    enc_slope,
    dec_edges,
    grid_part,
    mesh_back,
    tile_out,
    part_out,
    landed,
    enc_columns,
    dec_columns,
    send_sem,
    recv_sem,
):
    lat = lax.axis_index("lat")
    lon = lax.axis_index("lon")
    grid_rows, width = grid_feat.shape
    mesh_rows = mesh_feat.shape[0]
    enc_cap = enc_send.shape[2]
    dec_cap = dec_send.shape[2]
    turns = (4, 3, 5, 1, 7, 0, 2, 6, 8)
    others = turns[1:]

    def block_at(turn):
        k = turns[0]
        for i in range(1, 9):
            k = jnp.where(turn == i, turns[i], k)
        return k

    def inside(k):
        band = lat + k // 3 - 1
        return (band >= 0) & (band < n_lat)

    def peer(k):
        return (lat + k // 3 - 1, lax.rem(lon + k % 3 - 1 + n_lon, n_lon))

    def copy_of(stage, source, k):
        return pltpu.make_async_remote_copy(
            src_ref=source,
            dst_ref=landed.at[stage, 8 - k],
            send_sem=send_sem.at[stage, k],
            recv_sem=recv_sem.at[stage, 8 - k],
            device_id=peer(k),
            device_id_type=MESH,
        )

    def spread(stage, source):
        for k in others:

            @pl.when(inside(k))
            def _():
                copy_of(stage, source, k).start()

    def fold_out(stage, part, k):
        @pl.when((k != 4) & inside(k))
        def _():
            copy_of(stage, part_out.at[part, k], k).start()

    def arrived_one(stage, source, k):
        @pl.when((k != 4) & inside(k))
        def _():
            copy_of(stage, source, 8 - k).wait_recv()

    def arrived(stage, source):
        for k in others:

            @pl.when(inside(k))
            def _():
                copy_of(stage, source, 8 - k).wait_recv()

    def folded(stage, part):
        arrived(stage, part_out.at[part, 0])
        total = part_out[part, 4].astype(F32)
        for k in others:
            total = total + landed[stage, k].astype(F32)
        return total.astype(BF16)

    barrier = pltpu.get_barrier_semaphore()
    for k in others:

        @pl.when(inside(k))
        def _():
            pl.semaphore_signal(barrier, inc=1, device_id=peer(k), device_id_type=MESH)

    missing = jnp.where(lat == 0, 3, 0) + jnp.where(lat == n_lat - 1, 3, 0)
    pl.semaphore_wait(barrier, 8 - missing)

    spread(0, mesh_feat)

    lay_columns(enc_send, enc_columns, 0)
    lay_columns(enc_recv, enc_columns, 1)
    lay_columns(dec_send, dec_columns, 0)
    lay_columns(dec_recv, dec_columns, 1)

    for k in (0, 1, 2, 6, 7, 8):

        @pl.when(jnp.logical_not(inside(k)))
        def _():
            for stage in range(6):
                landed[stage, k] = jnp.zeros((mesh_rows, width), BF16)

    landed[0, 4] = mesh_feat[...]

    chunk = min(256, grid_rows)

    def rows_at(i, size):
        return pl.ds(pl.multiple_of(i * size, size), size)

    def project(i, _):
        rows = rows_at(i, chunk)
        enc_table[rows, :] = mm(grid_feat[rows, :], enc_src[...]).astype(BF16)
        dec_table[rows, :width] = mm(grid_feat[rows, :], dec_dst[...]).astype(BF16)
        dec_table[rows, width:] = mm_t(grid_cot[rows, :], dec_out[...]).astype(BF16)
        return 0

    lax.fori_loop(0, grid_rows // chunk, project, 0)

    def enc_gather(k, _):
        picks = pick_columns(column_of(enc_columns, 0, k), grid_rows)
        enc_edges[rows_at(k, enc_cap), :] = mm(picks, enc_table[...]).astype(BF16)
        return 0

    lax.fori_loop(0, 9, enc_gather, 0)

    def enc_forward(turn, _):
        k = block_at(turn)
        arrived_one(0, mesh_feat, k)
        rows = rows_at(k, enc_cap)
        side = mm(landed[0, k], enc_dst[...])
        high = side.astype(BF16)
        low = (side - high.astype(F32)).astype(BF16)
        picks = pick_columns(column_of(enc_columns, 1, k), mesh_rows)
        near = mm(picks, high) + mm(picks, low)
        pre = enc_edges[rows, :].astype(F32) + near + enc_bias[...]
        gate = gate_of(pre)
        message = pre * gate
        enc_slope[rows, :] = gate + message * (1.0 - gate)
        targets = pick_rows(live_row(enc_recv, enc_count, k), mesh_rows)
        part_out[0, k] = mm(targets, message.astype(BF16)).astype(BF16)
        fold_out(1, 0, k)
        return 0

    lax.fori_loop(0, 9, enc_forward, 0)

    def dec_gather(k, _):
        picks = pick_columns(column_of(dec_columns, 1, k), grid_rows)
        dec_edges[rows_at(k, dec_cap), :] = mm(picks, dec_table[...]).astype(BF16)
        return 0

    lax.fori_loop(0, 5, dec_gather, 0)

    enc_sum = folded(1, 0)
    mesh_new = (mesh_feat[...].astype(F32) + mm(enc_sum, enc_out[...])).astype(BF16)
    dec_proj = mm(mesh_new, dec_src[...]).astype(BF16)
    tile_out[0] = dec_proj
    landed[2, 4] = dec_proj
    spread(2, tile_out.at[0])

    lax.fori_loop(5, 9, dec_gather, 0)

    step = min(256, dec_cap)

    def dec_forward(turn, _):
        k = block_at(turn)
        arrived_one(2, tile_out.at[0], k)
        near_picks = pick_columns(column_of(dec_columns, 0, k), mesh_rows)
        near = landed[2, k]
        for first in range(0, dec_cap, step):
            rows = pl.ds(pl.multiple_of(k * dec_cap + first, step), step)
            pre = (
                mm(near_picks[first : first + step], near)
                + dec_edges[rows, :width].astype(F32)
                + dec_bias[...]
            )
            gate = gate_of(pre)
            message = pre * gate
            slope = gate + message * (1.0 - gate)
            back = dec_edges[rows, width:].astype(F32)
            dec_edges[rows, :width] = message.astype(BF16)
            dec_edges[rows, width:] = (back * slope).astype(BF16)
        targets = pick_rows(live_row(dec_send, dec_count, k), mesh_rows)
        part_out[1, k] = mm(targets, dec_edges[rows_at(k, dec_cap), width:]).astype(BF16)
        fold_out(3, 1, k)
        return 0

    lax.fori_loop(0, 9, dec_forward, 0)

    def dec_scatter(i, _):
        rows = rows_at(i, chunk)
        targets = jnp.concatenate(
            [pick_rows(live_row(dec_recv, dec_count, k), chunk, i * chunk) for k in range(9)], axis=1
        )
        summed = mm(targets, dec_edges[...]).astype(BF16)
        grid_new[rows, :] = (
            grid_feat[rows, :].astype(F32) + mm(summed[:, :width], dec_out[...])
        ).astype(BF16)
        grid_part[rows, :] = grid_cot[rows, :].astype(F32) + mm_t(summed[:, width:], dec_dst[...])
        return 0

    half = (grid_rows // chunk + 1) // 2
    lax.fori_loop(0, half, dec_scatter, 0)

    back = mm_t(folded(3, 1), dec_src[...])
    mesh_back[...] = back
    enc_back = mm_t(back.astype(BF16), enc_out[...]).astype(BF16)
    tile_out[1] = enc_back
    landed[4, 4] = enc_back
    spread(4, tile_out.at[1])

    lax.fori_loop(half, grid_rows // chunk, dec_scatter, 0)

    def enc_backward(turn, _):
        k = block_at(turn)
        arrived_one(4, tile_out.at[1], k)
        rows = rows_at(k, enc_cap)
        picks = pick_columns(column_of(enc_columns, 1, k), mesh_rows)
        grad = (mm(picks, landed[4, k]) * enc_slope[rows, :]).astype(BF16)
        enc_edges[rows, :] = grad
        targets = pick_rows(live_row(enc_recv, enc_count, k), mesh_rows)
        part_out[2, k] = mm(targets, grad).astype(BF16)
        fold_out(5, 2, k)
        return 0

    lax.fori_loop(0, 9, enc_backward, 0)

    def enc_scatter(i, _):
        rows = rows_at(i, chunk)
        targets = jnp.concatenate(
            [pick_rows(live_row(enc_send, enc_count, k), chunk, i * chunk) for k in range(9)], axis=1
        )
        summed = mm(targets, enc_edges[...]).astype(BF16)
        grid_grad[rows, :] = (grid_part[rows, :] + mm_t(summed, enc_src[...])).astype(BF16)
        return 0

    lax.fori_loop(0, grid_rows // chunk, enc_scatter, 0)

    mesh_grad[...] = (mesh_back[...] + mm_t(folded(5, 2), enc_dst[...])).astype(BF16)

    for k in others:

        @pl.when(inside(k))
        def _():
            copy_of(0, mesh_feat, k).wait_send()
            copy_of(1, part_out.at[0, k], k).wait_send()
            copy_of(2, tile_out.at[0], k).wait_send()
            copy_of(3, part_out.at[1, k], k).wait_send()
            copy_of(4, tile_out.at[1], k).wait_send()
            copy_of(5, part_out.at[2, k], k).wait_send()


def on_device(
    n_lat,
    n_lon,
    grid_feat,
    mesh_feat,
    enc_send,
    enc_recv,
    enc_count,
    dec_send,
    dec_recv,
    dec_count,
    enc_src,
    enc_dst,
    enc_bias,
    enc_out,
    dec_src,
    dec_dst,
    dec_bias,
    dec_out,
    grid_cot,
):
    grid_rows, width = grid_feat.shape
    mesh_rows = mesh_feat.shape[0]
    enc_slots = 9 * enc_send.shape[2]
    dec_slots = 9 * dec_send.shape[2]
    vmem = pl.BlockSpec(memory_space=pltpu.VMEM)
    smem = pl.BlockSpec(memory_space=pltpu.SMEM)
    return pl.pallas_call(
        functools.partial(kernel, n_lat, n_lon),
        out_shape=(
            jax.ShapeDtypeStruct((grid_rows, width), BF16),
            jax.ShapeDtypeStruct((mesh_rows, width), BF16),
            jax.ShapeDtypeStruct((grid_rows, width), BF16),
        ),
        in_specs=[vmem] * 4 + [smem] + [vmem] * 2 + [smem] + [vmem] * 9,
        out_specs=(vmem, vmem, vmem),
        scratch_shapes=[
            pltpu.VMEM((grid_rows, width), BF16),
            pltpu.VMEM((grid_rows, 2 * width), BF16),
            pltpu.VMEM((enc_slots, width), BF16),
            pltpu.VMEM((enc_slots, width), F32),
            pltpu.VMEM((dec_slots, 2 * width), BF16),
            pltpu.VMEM((grid_rows, width), F32),
            pltpu.VMEM((mesh_rows, width), F32),
            pltpu.VMEM((2, mesh_rows, width), BF16),
            pltpu.VMEM((3, 9, mesh_rows, width), BF16),
            pltpu.VMEM((6, 9, mesh_rows, width), BF16),
            pltpu.VMEM((2, enc_send.shape[2], 16), F32),
            pltpu.VMEM((2, dec_send.shape[2], 16), F32),
            pltpu.SemaphoreType.DMA((6, 9)),
            pltpu.SemaphoreType.DMA((6, 9)),
        ],
        compiler_params=pltpu.CompilerParams(
            collective_id=0, has_side_effects=True, vmem_limit_bytes=60 * 1024 * 1024
        ),
    )(
        grid_feat,
        mesh_feat,
        jnp.transpose(enc_send, (1, 0, 2)),
        jnp.transpose(enc_recv, (1, 0, 2)),
        enc_count,
        jnp.transpose(dec_send, (1, 0, 2)),
        jnp.transpose(dec_recv, (1, 0, 2)),
        dec_count,
        enc_src,
        enc_dst,
        enc_bias[None, :],
        enc_out,
        dec_src,
        dec_dst,
        dec_bias[None, :],
        dec_out,
        grid_cot,
    )


def solution(mesh):
    owned2 = P(("lat", "lon"), None)
    owned3 = P(("lat", "lon"), None, None)
    placed = (owned2, owned2, owned3, owned3, owned2, owned3, owned3, owned2) + (P(),) * 8 + (owned2,)
    return jax.shard_map(
        functools.partial(on_device, mesh.shape["lat"], mesh.shape["lon"]),
        mesh=mesh,
        in_specs=placed,
        out_specs=(owned2, owned2, owned2),
        check_vma=False,
    )
```

```python
import functools

import jax
import jax.numpy as jnp
from jax import lax
from jax.experimental import pallas as pl
from jax.experimental.pallas import tpu as pltpu
from jax.sharding import PartitionSpec as P

F32 = jnp.float32
BF16 = jnp.bfloat16
MESH = pl.DeviceIdType.MESH


def mm(a, b):
    return jnp.dot(a, b, preferred_element_type=F32)


def mm_t(a, b):
    return lax.dot_general(a, b, (((1,), (1,)), ((), ())), preferred_element_type=F32)


def lane_row(width):
    return lax.broadcasted_iota(jnp.int32, (1, width), 1)


def ones_where(mask):
    return jnp.where(mask, 1.0, 0.0).astype(BF16)


def pick_columns(column, row_count):
    return ones_where(column == lane_row(row_count).astype(F32))


def pick_rows(indices, row_count, base=0):
    rows = lax.broadcasted_iota(jnp.int32, (row_count, 1), 0) + base
    return ones_where(rows == indices)


def lay_columns(index_ref, columns_ref, at):
    blocks, _, slots = index_ref.shape
    rows = [index_ref[k].astype(F32) for k in range(blocks)]
    rows.append(jnp.zeros((16 - blocks, slots), F32))
    columns_ref[at] = jnp.concatenate(rows, axis=0).T


def column_of(columns_ref, which, at):
    columns = columns_ref[which]
    lane = lax.broadcasted_iota(jnp.int32, columns.shape, 1)
    return jnp.sum(jnp.where(lane == at, columns, 0.0), axis=1, keepdims=True)


def live_row(index_ref, count_ref, k):
    indices = index_ref[k]
    return jnp.where(lane_row(indices.shape[1]) < count_ref[0, k], indices, -1)


def gate_of(pre):
    return 0.5 * jnp.tanh(0.5 * pre) + 0.5


def kernel(
    n_lat,
    n_lon,
    grid_feat,
    mesh_feat,
    enc_send,
    enc_recv,
    enc_count,
    dec_send,
    dec_recv,
    dec_count,
    enc_src,
    enc_dst,
    enc_bias,
    enc_out,
    dec_src,
    dec_dst,
    dec_bias,
    dec_out,
    grid_cot,
    grid_new,
    mesh_grad,
    grid_grad,
    enc_table,
    dec_table,
    enc_edges,
    enc_slope,
    dec_edges,
    grid_part,
    mesh_back,
    tile_out,
    part_out,
    landed,
    enc_columns,
    dec_columns,
    send_sem,
    recv_sem,
):
    lat = lax.axis_index("lat")
    lon = lax.axis_index("lon")
    grid_rows, width = grid_feat.shape
    mesh_rows = mesh_feat.shape[0]
    enc_cap = enc_send.shape[2]
    dec_cap = dec_send.shape[2]
    turns = (4, 3, 5, 1, 7, 0, 2, 6, 8)
    others = turns[1:]

    def block_at(turn):
        k = turns[0]
        for i in range(1, 9):
            k = jnp.where(turn == i, turns[i], k)
        return k

    def inside(k):
        band = lat + k // 3 - 1
        return (band >= 0) & (band < n_lat)

    def peer(k):
        return (lat + k // 3 - 1, lax.rem(lon + k % 3 - 1 + n_lon, n_lon))

    def copy_of(stage, source, k):
        return pltpu.make_async_remote_copy(
            src_ref=source,
            dst_ref=landed.at[stage, 8 - k],
            send_sem=send_sem.at[stage, k],
            recv_sem=recv_sem.at[stage, 8 - k],
            device_id=peer(k),
            device_id_type=MESH,
        )

    def spread(stage, source):
        for k in (1, 7, 3, 5):

            @pl.when(inside(k))
            def _():
                copy_of(stage, source, k).start()

    def pass_on(stage, source):
        for k in (1, 7):

            @pl.when(inside(k))
            def _():
                copy_of(stage, source, 8 - k).wait_recv()
                for corner, side in ((k - 1, 1), (k + 1, n_lon - 1)):
                    pltpu.make_async_remote_copy(
                        src_ref=landed.at[stage, k],
                        dst_ref=landed.at[stage, corner],
                        send_sem=send_sem.at[stage, corner],
                        recv_sem=recv_sem.at[stage, corner],
                        device_id=(lat, lax.rem(lon + side, n_lon)),
                        device_id_type=MESH,
                    ).start()

    def fold_out(stage, part, k):
        @pl.when((k != 4) & inside(k))
        def _():
            copy_of(stage, part_out.at[part, k], k).start()

    def arrived_one(stage, source, k):
        @pl.when((k != 4) & (k != 1) & (k != 7) & inside(k))
        def _():
            copy_of(stage, source, 8 - k).wait_recv()

    def arrived(stage, source):
        for k in others:

            @pl.when(inside(k))
            def _():
                copy_of(stage, source, 8 - k).wait_recv()

    def folded(stage, part):
        arrived(stage, part_out.at[part, 0])
        total = part_out[part, 4].astype(F32)
        for k in others:
            total = total + landed[stage, k].astype(F32)
        return total.astype(BF16)

    barrier = pltpu.get_barrier_semaphore()
    for k in others:

        @pl.when(inside(k))
        def _():
            pl.semaphore_signal(barrier, inc=1, device_id=peer(k), device_id_type=MESH)

    missing = jnp.where(lat == 0, 3, 0) + jnp.where(lat == n_lat - 1, 3, 0)
    pl.semaphore_wait(barrier, 8 - missing)

    spread(0, mesh_feat)

    lay_columns(enc_send, enc_columns, 0)
    lay_columns(enc_recv, enc_columns, 1)
    lay_columns(dec_send, dec_columns, 0)
    lay_columns(dec_recv, dec_columns, 1)

    for k in (0, 1, 2, 6, 7, 8):

        @pl.when(jnp.logical_not(inside(k)))
        def _():
            for stage in range(6):
                landed[stage, k] = jnp.zeros((mesh_rows, width), BF16)

    landed[0, 4] = mesh_feat[...]

    chunk = min(256, grid_rows)

    def rows_at(i, size):
        return pl.ds(pl.multiple_of(i * size, size), size)

    def project(i, _):
        rows = rows_at(i, chunk)
        enc_table[rows, :] = mm(grid_feat[rows, :], enc_src[...]).astype(BF16)
        dec_table[rows, :width] = mm(grid_feat[rows, :], dec_dst[...]).astype(BF16)
        dec_table[rows, width:] = mm_t(grid_cot[rows, :], dec_out[...]).astype(BF16)
        return 0

    lax.fori_loop(0, grid_rows // chunk, project, 0)

    def enc_gather(k, _):
        picks = pick_columns(column_of(enc_columns, 0, k), grid_rows)
        enc_edges[rows_at(k, enc_cap), :] = mm(picks, enc_table[...]).astype(BF16)
        return 0

    lax.fori_loop(0, 9, enc_gather, 0)

    def enc_forward(turn, _):
        k = block_at(turn)
        arrived_one(0, mesh_feat, k)
        rows = rows_at(k, enc_cap)
        side = mm(landed[0, k], enc_dst[...])
        high = side.astype(BF16)
        low = (side - high.astype(F32)).astype(BF16)
        picks = pick_columns(column_of(enc_columns, 1, k), mesh_rows)
        near = mm(picks, high) + mm(picks, low)
        pre = enc_edges[rows, :].astype(F32) + near + enc_bias[...]
        gate = gate_of(pre)
        message = pre * gate
        enc_slope[rows, :] = gate + message * (1.0 - gate)
        targets = pick_rows(live_row(enc_recv, enc_count, k), mesh_rows)
        part_out[0, k] = mm(targets, message.astype(BF16)).astype(BF16)
        fold_out(1, 0, k)
        return 0

    pass_on(0, mesh_feat)
    lax.fori_loop(0, 9, enc_forward, 0)

    def dec_gather(k, _):
        picks = pick_columns(column_of(dec_columns, 1, k), grid_rows)
        dec_edges[rows_at(k, dec_cap), :] = mm(picks, dec_table[...]).astype(BF16)
        return 0

    lax.fori_loop(0, 5, dec_gather, 0)

    enc_sum = folded(1, 0)
    mesh_new = (mesh_feat[...].astype(F32) + mm(enc_sum, enc_out[...])).astype(BF16)
    dec_proj = mm(mesh_new, dec_src[...]).astype(BF16)
    tile_out[0] = dec_proj
    landed[2, 4] = dec_proj
    spread(2, tile_out.at[0])

    lax.fori_loop(5, 9, dec_gather, 0)

    step = min(256, dec_cap)

    def dec_forward(turn, _):
        k = block_at(turn)
        arrived_one(2, tile_out.at[0], k)
        near_picks = pick_columns(column_of(dec_columns, 0, k), mesh_rows)
        near = landed[2, k]
        for first in range(0, dec_cap, step):
            rows = pl.ds(pl.multiple_of(k * dec_cap + first, step), step)
            pre = (
                mm(near_picks[first : first + step], near)
                + dec_edges[rows, :width].astype(F32)
                + dec_bias[...]
            )
            gate = gate_of(pre)
            message = pre * gate
            slope = gate + message * (1.0 - gate)
            back = dec_edges[rows, width:].astype(F32)
            dec_edges[rows, :width] = message.astype(BF16)
            dec_edges[rows, width:] = (back * slope).astype(BF16)
        targets = pick_rows(live_row(dec_send, dec_count, k), mesh_rows)
        part_out[1, k] = mm(targets, dec_edges[rows_at(k, dec_cap), width:]).astype(BF16)
        fold_out(3, 1, k)
        return 0

    pass_on(2, tile_out.at[0])
    lax.fori_loop(0, 9, dec_forward, 0)

    def dec_scatter(i, _):
        rows = rows_at(i, chunk)
        targets = jnp.concatenate(
            [pick_rows(live_row(dec_recv, dec_count, k), chunk, i * chunk) for k in range(9)], axis=1
        )
        summed = mm(targets, dec_edges[...]).astype(BF16)
        grid_new[rows, :] = (
            grid_feat[rows, :].astype(F32) + mm(summed[:, :width], dec_out[...])
        ).astype(BF16)
        grid_part[rows, :] = grid_cot[rows, :].astype(F32) + mm_t(summed[:, width:], dec_dst[...])
        return 0

    half = (grid_rows // chunk + 1) // 2
    lax.fori_loop(0, half, dec_scatter, 0)

    back = mm_t(folded(3, 1), dec_src[...])
    mesh_back[...] = back
    enc_back = mm_t(back.astype(BF16), enc_out[...]).astype(BF16)
    tile_out[1] = enc_back
    landed[4, 4] = enc_back
    spread(4, tile_out.at[1])

    most = (half + grid_rows // chunk) // 2
    lax.fori_loop(half, most, dec_scatter, 0)

    def enc_backward(turn, _):
        k = block_at(turn)
        arrived_one(4, tile_out.at[1], k)
        rows = rows_at(k, enc_cap)
        picks = pick_columns(column_of(enc_columns, 1, k), mesh_rows)
        grad = (mm(picks, landed[4, k]) * enc_slope[rows, :]).astype(BF16)
        enc_edges[rows, :] = grad
        targets = pick_rows(live_row(enc_recv, enc_count, k), mesh_rows)
        part_out[2, k] = mm(targets, grad).astype(BF16)
        fold_out(5, 2, k)
        return 0

    pass_on(4, tile_out.at[1])
    lax.fori_loop(0, 9, enc_backward, 0)

    def enc_scatter(i, _):
        rows = rows_at(i, chunk)
        targets = jnp.concatenate(
            [pick_rows(live_row(enc_send, enc_count, k), chunk, i * chunk) for k in range(9)], axis=1
        )
        summed = mm(targets, enc_edges[...]).astype(BF16)
        grid_grad[rows, :] = (grid_part[rows, :] + mm_t(summed, enc_src[...])).astype(BF16)
        return 0

    lax.fori_loop(most, grid_rows // chunk, dec_scatter, 0)
    lax.fori_loop(0, grid_rows // chunk, enc_scatter, 0)

    mesh_grad[...] = (mesh_back[...] + mm_t(folded(5, 2), enc_dst[...])).astype(BF16)

    for k in others:

        @pl.when(inside(k))
        def _():
            copy_of(0, mesh_feat, k).wait_send()
            copy_of(1, part_out.at[0, k], k).wait_send()
            copy_of(2, tile_out.at[0], k).wait_send()
            copy_of(3, part_out.at[1, k], k).wait_send()
            copy_of(4, tile_out.at[1], k).wait_send()
            copy_of(5, part_out.at[2, k], k).wait_send()


def on_device(
    n_lat,
    n_lon,
    grid_feat,
    mesh_feat,
    enc_send,
    enc_recv,
    enc_count,
    dec_send,
    dec_recv,
    dec_count,
    enc_src,
    enc_dst,
    enc_bias,
    enc_out,
    dec_src,
    dec_dst,
    dec_bias,
    dec_out,
    grid_cot,
):
    grid_rows, width = grid_feat.shape
    mesh_rows = mesh_feat.shape[0]
    enc_slots = 9 * enc_send.shape[2]
    dec_slots = 9 * dec_send.shape[2]
    vmem = pl.BlockSpec(memory_space=pltpu.VMEM)
    smem = pl.BlockSpec(memory_space=pltpu.SMEM)
    return pl.pallas_call(
        functools.partial(kernel, n_lat, n_lon),
        out_shape=(
            jax.ShapeDtypeStruct((grid_rows, width), BF16),
            jax.ShapeDtypeStruct((mesh_rows, width), BF16),
            jax.ShapeDtypeStruct((grid_rows, width), BF16),
        ),
        in_specs=[vmem] * 4 + [smem] + [vmem] * 2 + [smem] + [vmem] * 9,
        out_specs=(vmem, vmem, vmem),
        scratch_shapes=[
            pltpu.VMEM((grid_rows, width), BF16),
            pltpu.VMEM((grid_rows, 2 * width), BF16),
            pltpu.VMEM((enc_slots, width), BF16),
            pltpu.VMEM((enc_slots, width), F32),
            pltpu.VMEM((dec_slots, 2 * width), BF16),
            pltpu.VMEM((grid_rows, width), F32),
            pltpu.VMEM((mesh_rows, width), F32),
            pltpu.VMEM((2, mesh_rows, width), BF16),
            pltpu.VMEM((3, 9, mesh_rows, width), BF16),
            pltpu.VMEM((6, 9, mesh_rows, width), BF16),
            pltpu.VMEM((2, enc_send.shape[2], 16), F32),
            pltpu.VMEM((2, dec_send.shape[2], 16), F32),
            pltpu.SemaphoreType.DMA((6, 9)),
            pltpu.SemaphoreType.DMA((6, 9)),
        ],
        compiler_params=pltpu.CompilerParams(
            collective_id=0, has_side_effects=True, vmem_limit_bytes=60 * 1024 * 1024
        ),
    )(
        grid_feat,
        mesh_feat,
        jnp.transpose(enc_send, (1, 0, 2)),
        jnp.transpose(enc_recv, (1, 0, 2)),
        enc_count,
        jnp.transpose(dec_send, (1, 0, 2)),
        jnp.transpose(dec_recv, (1, 0, 2)),
        dec_count,
        enc_src,
        enc_dst,
        enc_bias[None, :],
        enc_out,
        dec_src,
        dec_dst,
        dec_bias[None, :],
        dec_out,
        grid_cot,
    )


def solution(mesh):
    owned2 = P(("lat", "lon"), None)
    owned3 = P(("lat", "lon"), None, None)
    placed = (owned2, owned2, owned3, owned3, owned2, owned3, owned3, owned2) + (P(),) * 8 + (owned2,)
    return jax.shard_map(
        functools.partial(on_device, mesh.shape["lat"], mesh.shape["lon"]),
        mesh=mesh,
        in_specs=placed,
        out_specs=(owned2, owned2, owned2),
        check_vma=False,
    )
```

```python
import functools

import jax
import jax.numpy as jnp
from jax import lax
from jax.experimental import pallas as pl
from jax.experimental.pallas import tpu as pltpu
from jax.sharding import PartitionSpec as P

F32 = jnp.float32
BF16 = jnp.bfloat16
MESH = pl.DeviceIdType.MESH


def mm(a, b):
    return jnp.dot(a, b, preferred_element_type=F32)


def mm_t(a, b):
    return lax.dot_general(a, b, (((1,), (1,)), ((), ())), preferred_element_type=F32)


def lane_row(width):
    return lax.broadcasted_iota(jnp.int32, (1, width), 1)


def ones_where(mask):
    return jnp.where(mask, 1.0, 0.0).astype(BF16)


def pick_columns(column, row_count):
    return ones_where(column == lane_row(row_count).astype(F32))


def pick_rows(indices, row_count, base=0):
    rows = lax.broadcasted_iota(jnp.int32, (row_count, 1), 0) + base
    return ones_where(rows == indices)


def lay_columns(index_ref, columns_ref, at):
    blocks, _, slots = index_ref.shape
    rows = [index_ref[k].astype(F32) for k in range(blocks)]
    rows.append(jnp.zeros((16 - blocks, slots), F32))
    columns_ref[at] = jnp.concatenate(rows, axis=0).T


def column_of(columns_ref, which, at):
    columns = columns_ref[which]
    lane = lax.broadcasted_iota(jnp.int32, columns.shape, 1)
    return jnp.sum(jnp.where(lane == at, columns, 0.0), axis=1, keepdims=True)


def live_row(index_ref, count_ref, k):
    indices = index_ref[k]
    return jnp.where(lane_row(indices.shape[1]) < count_ref[0, k], indices, -1)


def gate_of(pre):
    return 0.5 * jnp.tanh(0.5 * pre) + 0.5


def kernel(
    n_lat,
    n_lon,
    grid_feat,
    mesh_feat,
    enc_send,
    enc_recv,
    enc_count,
    dec_send,
    dec_recv,
    dec_count,
    enc_src,
    enc_dst,
    enc_bias,
    enc_out,
    dec_src,
    dec_dst,
    dec_bias,
    dec_out,
    grid_cot,
    grid_new,
    mesh_grad,
    grid_grad,
    enc_table,
    dec_table,
    enc_edges,
    enc_slope,
    dec_edges,
    grid_part,
    mesh_back,
    tile_out,
    part_out,
    landed,
    enc_columns,
    dec_columns,
    send_sem,
    recv_sem,
):
    lat = lax.axis_index("lat")
    lon = lax.axis_index("lon")
    grid_rows, width = grid_feat.shape
    mesh_rows = mesh_feat.shape[0]
    enc_cap = enc_send.shape[2]
    dec_cap = dec_send.shape[2]
    turns = (4, 3, 5, 1, 7, 0, 2, 6, 8)
    others = turns[1:]

    def block_at(turn):
        k = turns[0]
        for i in range(1, 9):
            k = jnp.where(turn == i, turns[i], k)
        return k

    def inside(k):
        band = lat + k // 3 - 1
        return (band >= 0) & (band < n_lat)

    def peer(k):
        return (lat + k // 3 - 1, lax.rem(lon + k % 3 - 1 + n_lon, n_lon))

    def copy_of(stage, source, k):
        return pltpu.make_async_remote_copy(
            src_ref=source,
            dst_ref=landed.at[stage, 8 - k],
            send_sem=send_sem.at[stage, k],
            recv_sem=recv_sem.at[stage, 8 - k],
            device_id=peer(k),
            device_id_type=MESH,
        )

    def spread(stage, source):
        for k in (1, 7, 3, 5):

            @pl.when(inside(k))
            def _():
                copy_of(stage, source, k).start()

    def pass_on(stage, source):
        for k in (1, 7):

            @pl.when(inside(k))
            def _():
                copy_of(stage, source, 8 - k).wait_recv()
                for corner, side in ((k - 1, 1), (k + 1, n_lon - 1)):
                    pltpu.make_async_remote_copy(
                        src_ref=landed.at[stage, k],
                        dst_ref=landed.at[stage, corner],
                        send_sem=send_sem.at[stage, corner],
                        recv_sem=recv_sem.at[stage, corner],
                        device_id=(lat, lax.rem(lon + side, n_lon)),
                        device_id_type=MESH,
                    ).start()

    def fold_out(stage, part, k):
        @pl.when((k != 4) & inside(k))
        def _():
            copy_of(stage, part_out.at[part, k], k).start()

    def arrived_one(stage, source, k):
        @pl.when((k != 4) & (k != 1) & (k != 7) & inside(k))
        def _():
            copy_of(stage, source, 8 - k).wait_recv()

    def arrived(stage, source):
        for k in others:

            @pl.when(inside(k))
            def _():
                copy_of(stage, source, 8 - k).wait_recv()

    def folded(stage, part):
        arrived(stage, part_out.at[part, 0])
        total = part_out[part, 4].astype(F32)
        for k in others:
            total = total + landed[stage, k].astype(F32)
        return total.astype(BF16)

    barrier = pltpu.get_barrier_semaphore()
    for k in others:

        @pl.when(inside(k))
        def _():
            pl.semaphore_signal(barrier, inc=1, device_id=peer(k), device_id_type=MESH)

    missing = jnp.where(lat == 0, 3, 0) + jnp.where(lat == n_lat - 1, 3, 0)
    pl.semaphore_wait(barrier, 8 - missing)

    spread(0, mesh_feat)

    lay_columns(enc_send, enc_columns, 0)
    lay_columns(enc_recv, enc_columns, 1)
    lay_columns(dec_send, dec_columns, 0)
    lay_columns(dec_recv, dec_columns, 1)

    for k in (0, 1, 2, 6, 7, 8):

        @pl.when(jnp.logical_not(inside(k)))
        def _():
            for stage in range(6):
                landed[stage, k] = jnp.zeros((mesh_rows, width), BF16)

    landed[0, 4] = mesh_feat[...]

    chunk = min(256, grid_rows)

    def rows_at(i, size):
        return pl.ds(pl.multiple_of(i * size, size), size)

    def project(i, _):
        rows = rows_at(i, chunk)
        enc_table[rows, :] = mm(grid_feat[rows, :], enc_src[...]).astype(BF16)
        dec_table[rows, :width] = mm(grid_feat[rows, :], dec_dst[...]).astype(BF16)
        dec_table[rows, width:] = mm_t(grid_cot[rows, :], dec_out[...]).astype(BF16)
        return 0

    lax.fori_loop(0, grid_rows // chunk, project, 0)

    def enc_gather(k, _):
        picks = pick_columns(column_of(enc_columns, 0, k), grid_rows)
        enc_edges[rows_at(k, enc_cap), :] = mm(picks, enc_table[...]).astype(BF16)
        return 0

    lax.fori_loop(0, 9, enc_gather, 0)

    def enc_forward(turn, _):
        k = block_at(turn)
        arrived_one(0, mesh_feat, k)
        rows = rows_at(k, enc_cap)
        side = mm(landed[0, k], enc_dst[...])
        high = side.astype(BF16)
        low = (side - high.astype(F32)).astype(BF16)
        picks = pick_columns(column_of(enc_columns, 1, k), mesh_rows)
        near = mm(picks, high) + mm(picks, low)
        pre = enc_edges[rows, :].astype(F32) + near + enc_bias[...]
        gate = gate_of(pre)
        message = pre * gate
        enc_slope[rows, :] = gate + message * (1.0 - gate)
        targets = pick_rows(live_row(enc_recv, enc_count, k), mesh_rows)
        part_out[0, k] = mm(targets, message.astype(BF16)).astype(BF16)
        fold_out(1, 0, k)
        return 0

    pass_on(0, mesh_feat)
    lax.fori_loop(0, 9, enc_forward, 0)

    def dec_gather(k, _):
        picks = pick_columns(column_of(dec_columns, 1, k), grid_rows)
        dec_edges[rows_at(k, dec_cap), :] = mm(picks, dec_table[...]).astype(BF16)
        return 0

    lax.fori_loop(0, 5, dec_gather, 0)

    enc_sum = folded(1, 0)
    mesh_new = (mesh_feat[...].astype(F32) + mm(enc_sum, enc_out[...])).astype(BF16)
    dec_proj = mm(mesh_new, dec_src[...]).astype(BF16)
    tile_out[0] = dec_proj
    landed[2, 4] = dec_proj
    spread(2, tile_out.at[0])

    lax.fori_loop(5, 9, dec_gather, 0)

    step = min(256, dec_cap)

    def dec_forward(turn, _):
        k = block_at(turn)
        arrived_one(2, tile_out.at[0], k)
        near_picks = pick_columns(column_of(dec_columns, 0, k), mesh_rows)
        near = landed[2, k]
        for first in range(0, dec_cap, step):
            rows = pl.ds(pl.multiple_of(k * dec_cap + first, step), step)
            pre = (
                mm(near_picks[first : first + step], near)
                + dec_edges[rows, :width].astype(F32)
                + dec_bias[...]
            )
            gate = gate_of(pre)
            message = pre * gate
            slope = gate + message * (1.0 - gate)
            back = dec_edges[rows, width:].astype(F32)
            dec_edges[rows, :width] = message.astype(BF16)
            dec_edges[rows, width:] = (back * slope).astype(BF16)
        targets = pick_rows(live_row(dec_send, dec_count, k), mesh_rows)
        part_out[1, k] = mm(targets, dec_edges[rows_at(k, dec_cap), width:]).astype(BF16)
        fold_out(3, 1, k)
        return 0

    pass_on(2, tile_out.at[0])
    lax.fori_loop(0, 9, dec_forward, 0)

    def dec_scatter(i, _):
        rows = rows_at(i, chunk)
        targets = jnp.concatenate(
            [pick_rows(live_row(dec_recv, dec_count, k), chunk, i * chunk) for k in range(9)], axis=1
        )
        summed = mm(targets, dec_edges[...]).astype(BF16)
        grid_new[rows, :] = (
            grid_feat[rows, :].astype(F32) + mm(summed[:, :width], dec_out[...])
        ).astype(BF16)
        grid_part[rows, :] = grid_cot[rows, :].astype(F32) + mm_t(summed[:, width:], dec_dst[...])
        return 0

    half = (grid_rows // chunk + 1) // 2
    lax.fori_loop(0, half, dec_scatter, 0)

    back = mm_t(folded(3, 1), dec_src[...])
    mesh_back[...] = back
    enc_back = mm_t(back.astype(BF16), enc_out[...]).astype(BF16)
    tile_out[1] = enc_back
    landed[4, 4] = enc_back
    spread(4, tile_out.at[1])

    most = (half + grid_rows // chunk) // 2
    lax.fori_loop(half, most, dec_scatter, 0)

    def enc_backward(turn, _):
        k = block_at(turn)
        arrived_one(4, tile_out.at[1], k)
        rows = rows_at(k, enc_cap)
        picks = pick_columns(column_of(enc_columns, 1, k), mesh_rows)
        grad = (mm(picks, landed[4, k]) * enc_slope[rows, :]).astype(BF16)
        enc_edges[rows, :] = grad
        targets = pick_rows(live_row(enc_recv, enc_count, k), mesh_rows)
        part_out[2, k] = mm(targets, grad).astype(BF16)
        fold_out(5, 2, k)
        return 0

    pass_on(4, tile_out.at[1])
    lax.fori_loop(0, 9, enc_backward, 0)

    def enc_scatter(i, _):
        rows = rows_at(i, chunk)
        targets = jnp.concatenate(
            [pick_rows(live_row(enc_send, enc_count, k), chunk, i * chunk) for k in range(9)], axis=1
        )
        summed = mm(targets, enc_edges[...]).astype(BF16)
        grid_grad[rows, :] = (grid_part[rows, :] + mm_t(summed, enc_src[...])).astype(BF16)
        return 0

    lax.fori_loop(most, grid_rows // chunk, dec_scatter, 0)
    lax.fori_loop(0, grid_rows // chunk, enc_scatter, 0)

    mesh_grad[...] = (mesh_back[...] + mm_t(folded(5, 2), enc_dst[...])).astype(BF16)

    for k in others:

        @pl.when(inside(k))
        def _():
            copy_of(0, mesh_feat, k).wait_send()
            copy_of(1, part_out.at[0, k], k).wait_send()
            copy_of(2, tile_out.at[0], k).wait_send()
            copy_of(3, part_out.at[1, k], k).wait_send()
            copy_of(4, tile_out.at[1], k).wait_send()
            copy_of(5, part_out.at[2, k], k).wait_send()


def settle(*refs):
    for source, target in zip(refs[:3], refs[3:]):
        target[...] = source[...]


def written_out(results, parts):
    blocks = [
        pl.BlockSpec((r.shape[0] // parts, r.shape[1]), lambda i: (i, 0)) for r in results
    ]
    return pl.pallas_call(
        settle,
        grid=(parts,),
        out_shape=tuple(jax.ShapeDtypeStruct(r.shape, r.dtype) for r in results),
        in_specs=blocks,
        out_specs=tuple(blocks),
    )(*results)


def on_device(
    n_lat,
    n_lon,
    grid_feat,
    mesh_feat,
    enc_send,
    enc_recv,
    enc_count,
    dec_send,
    dec_recv,
    dec_count,
    enc_src,
    enc_dst,
    enc_bias,
    enc_out,
    dec_src,
    dec_dst,
    dec_bias,
    dec_out,
    grid_cot,
):
    grid_rows, width = grid_feat.shape
    mesh_rows = mesh_feat.shape[0]
    enc_slots = 9 * enc_send.shape[2]
    dec_slots = 9 * dec_send.shape[2]
    vmem = pl.BlockSpec(memory_space=pltpu.VMEM)
    smem = pl.BlockSpec(memory_space=pltpu.SMEM)
    results = pl.pallas_call(
        functools.partial(kernel, n_lat, n_lon),
        out_shape=(
            jax.ShapeDtypeStruct((grid_rows, width), BF16),
            jax.ShapeDtypeStruct((mesh_rows, width), BF16),
            jax.ShapeDtypeStruct((grid_rows, width), BF16),
        ),
        in_specs=[vmem] * 4 + [smem] + [vmem] * 2 + [smem] + [vmem] * 9,
        out_specs=(vmem, vmem, vmem),
        scratch_shapes=[
            pltpu.VMEM((grid_rows, width), BF16),
            pltpu.VMEM((grid_rows, 2 * width), BF16),
            pltpu.VMEM((enc_slots, width), BF16),
            pltpu.VMEM((enc_slots, width), F32),
            pltpu.VMEM((dec_slots, 2 * width), BF16),
            pltpu.VMEM((grid_rows, width), F32),
            pltpu.VMEM((mesh_rows, width), F32),
            pltpu.VMEM((2, mesh_rows, width), BF16),
            pltpu.VMEM((3, 9, mesh_rows, width), BF16),
            pltpu.VMEM((6, 9, mesh_rows, width), BF16),
            pltpu.VMEM((2, enc_send.shape[2], 16), F32),
            pltpu.VMEM((2, dec_send.shape[2], 16), F32),
            pltpu.SemaphoreType.DMA((6, 9)),
            pltpu.SemaphoreType.DMA((6, 9)),
        ],
        compiler_params=pltpu.CompilerParams(
            collective_id=0, has_side_effects=True, vmem_limit_bytes=60 * 1024 * 1024
        ),
    )(
        grid_feat,
        mesh_feat,
        jnp.transpose(enc_send, (1, 0, 2)),
        jnp.transpose(enc_recv, (1, 0, 2)),
        enc_count,
        jnp.transpose(dec_send, (1, 0, 2)),
        jnp.transpose(dec_recv, (1, 0, 2)),
        dec_count,
        enc_src,
        enc_dst,
        enc_bias[None, :],
        enc_out,
        dec_src,
        dec_dst,
        dec_bias[None, :],
        dec_out,
        grid_cot,
    )
    return written_out(results, 4)


def solution(mesh):
    owned2 = P(("lat", "lon"), None)
    owned3 = P(("lat", "lon"), None, None)
    placed = (owned2, owned2, owned3, owned3, owned2, owned3, owned3, owned2) + (P(),) * 8 + (owned2,)
    return jax.shard_map(
        functools.partial(on_device, mesh.shape["lat"], mesh.shape["lon"]),
        mesh=mesh,
        in_specs=placed,
        out_specs=(owned2, owned2, owned2),
        check_vma=False,
    )
```
